32 devices in a mesh: parts: 2 (over y), seq: 4 (over x, core), mp: 4 (over z).
Axes of the slice: x: 2, y: 2, z: 4, core: 2. Of those that a mesh axis runs over, the one named last changes fastest.
Arguments:
- tokens: bfloat16 [4096, 8192], P(('parts', 'seq'), 'mp'), parts along dimension 0, may hold values from -6 to 6
- w_in: bfloat16 [3, 8192, 512], P(None, 'seq', 'mp'), may hold values from -0.0625 to 0.0625
- short_filter: float32 [3, 3, 512], P(None, None, 'mp'), may hold values from -3 to 3
- long_filter: float32 [32, 128], P('mp'), may hold values from -0.5 to 0.5
- skip: float32 [512], P('mp'), may hold values from -4 to 4
Outputs:
- mixed: bfloat16 [4096, 512], P(('parts', 'seq'), 'mp'), parts along dimension 0
The draws below stay inside these ranges and needn't reach their ends.
There are 2 independent parts, one for each index of `parts`. The reference program is written for one: setup_inputs(seed, part) draws one part's arguments, and reference() takes and returns one part's arrays. A program takes and returns all parts, laid end to end along the dimension named above; an argument that names none is the same for every part. Nothing has to cross between parts.
All inputs are finite; a program needn't handle non-finite values.
Results may differ from the reference program's by a relative error of at most 0.0081.
Values may be sent and summed in bfloat16 or wider, within the bound.
A program may use at most 64 MiB of HBM per device.

```python
import jax
import jax.numpy as jnp
from jax import lax

D = 8192
FLT = 128
GRP = 16
CH = 512
GROUPS = 32
TOKENS = 2048


def level_of(own_key, extent, split, smallest, largest):
    level = 1.0
    for axis_at, blocks in split:
        draws = jax.random.uniform(jax.random.fold_in(jax.random.fold_in(own_key, 6), axis_at), (blocks,), jnp.float32, smallest / len(split), largest / len(split))
        level = level * jnp.repeat(jnp.exp(draws), extent[axis_at] // blocks).reshape((-1,) + (1,) * (len(extent) - 1 - axis_at))
    return level


def noise(stream_key, extent, spread, bound, split=(), dtype=jnp.bfloat16):
    level = level_of(stream_key, extent, split, -0.22, 0.18) if split else 1.0
    drawn = jax.random.normal(stream_key, extent, jnp.float32) * spread * level
    return jnp.minimum(jnp.maximum(drawn, -bound), bound).astype(dtype)


def setup_inputs(seed: int = 0, part: int = 0) -> dict:
    key_list = jax.random.split(jax.random.key(seed), 6)
    part_splits = jax.random.split(jax.random.fold_in(key_list[5], part), 6)
    tokens = noise(part_splits[0], (TOKENS, D), 1.0, 6.0, ((0, 4), (1, 4)))
    w_in = noise(key_list[1], (3, D, CH), D ** -0.5, 0.0625, ((1, 4), (2, 4)))
    short_filter = noise(key_list[2], (3, 3, CH), 0.6, 3.0, ((2, 4),), jnp.float32)
    long_filter = noise(key_list[3], (GROUPS, FLT), FLT ** -0.5, 0.5, ((0, 4),), jnp.float32)
    skip = noise(key_list[4], (CH,), 1.0, 4.0, ((0, 4),), jnp.float32)
    return dict(tokens=tokens, w_in=w_in, short_filter=short_filter, long_filter=long_filter, skip=skip)


def reference(tokens, w_in, short_filter, long_filter, skip):
    xf = tokens.astype(jnp.float32)
    ms = lax.optimization_barrier(jnp.mean(xf * xf, axis=1, keepdims=True))
    normed = (xf * lax.rsqrt(ms + 1e-06)).astype(jnp.bfloat16)
    proj = jnp.stack([jnp.dot(normed, w_in[p], preferred_element_type=jnp.float32) for p in range(3)]).astype(jnp.bfloat16)
    padded = jnp.pad(proj.astype(jnp.float32), ((0, 0), (2, 0), (0, 0)))
    sharp = jnp.zeros(proj.shape, jnp.float32)
    for j in range(3):
        sharp = sharp + short_filter[:, j, None, :] * padded[:, 2 - j:2 - j + TOKENS, :]
    gated = sharp[1] * sharp[2]
    taps = jnp.repeat(long_filter, GRP, axis=0).T
    zpad = jnp.pad(gated, ((FLT - 1, 0), (0, 0)))

    def add_tap(step, acc):
        step = jnp.asarray(step).astype(jnp.int32)
        weight = lax.dynamic_index_in_dim(taps, step, 0, keepdims=False)
        start = (FLT - 1 - step).astype(jnp.int32)
        return acc + weight * lax.dynamic_slice_in_dim(zpad, start, TOKENS, 0)
    filtered = lax.fori_loop(0, FLT, add_tap, skip[None, :] * gated)
    return (sharp[0] * filtered).astype(jnp.bfloat16)
```

```python
import functools

import jax
import jax.numpy as jnp
from jax import lax
from jax.experimental import pallas as pl
from jax.experimental.pallas import tpu as pltpu
from jax.sharding import PartitionSpec as P

FLT = 128
GRP = 16


def passed_along(block, axis, distance):
    devices = range(lax.axis_size(axis))
    route = [(i - distance, i) for i in devices if i - distance in devices]
    return lax.ppermute(block, axis, route)


def project(Y, S, M, x_ref, w_ref, out_ref, wbuf, pbuf, rbuf, pself, ssbuf,
            send1, send_a, recv_a, send_b, recv_b, send_p, recv_p, send_s, recv_s):
    X, R = S // 2, M // S
    T, F = x_ref.shape
    part_rows = F // Y
    y, s, m = lax.axis_index("parts"), lax.axis_index("seq"), lax.axis_index("mp")
    x, core = s // 2, s % 2

    def at(y_, s_, m_):
        return {"parts": y_, "seq": s_, "mp": m_}

    mq = m % S
    relay = 2 * (mq % X) + mq // X
    family = x + core * X

    def is_self(r):
        return jnp.logical_and(relay == s, R * s + r == m)

    def source_is_self(r2):
        return jnp.logical_and(m // R == s, family + S * r2 == m)

    def chunk(y_, x_, core_, r2):
        c = x_ + core_ * X + S * r2
        return wbuf.at[c, :, pl.ds(pl.multiple_of(y_ * part_rows, part_rows), part_rows), :]

    def arrived(ref, sem):
        pltpu.make_async_copy(ref, ref, sem).wait()

    others = [(dy, dx) for dx in range(X) for dy in range(Y) if dy or dx]

    def other(dy, dx):
        return (y + dy) % Y, (x + dx) % X

    barrier = pltpu.get_barrier_semaphore()

    def greet(dev):
        pl.semaphore_signal(barrier, inc=1, device_id=dev, device_id_type=pl.DeviceIdType.MESH)

    for r in range(R):
        @pl.when(jnp.logical_not(is_self(r)))
        def _(r=r):
            greet(at(y, relay, R * s + r))

        @pl.when(jnp.logical_not(source_is_self(r)))
        def _(r=r):
            greet(at(y, m // R, family + S * r))
    for dy, dx in others:
        yo, xo = other(dy, dx)
        greet(at(yo, 2 * xo + core, m))
    greet(at(y, 2 * x + 1 - core, m))
    for k in range(1, M):
        greet(at(y, s, (m + k) % M))
    peers = len(others) + 1 + M - 1 + 2 * R
    for r in range(R):
        peers = peers - is_self(r).astype(jnp.int32) - source_is_self(r).astype(jnp.int32)
    pl.semaphore_wait(barrier, peers)

    def first(r):
        rows = pl.ds(pl.multiple_of(r * F + y * part_rows, part_rows), part_rows)
        dst = wbuf.at[m, :, pl.ds(pl.multiple_of(y * part_rows, part_rows), part_rows), :]
        rx, rc = relay // 2, relay % 2
        sem = recv_a.at[y, rx, m // S]
        return w_ref.at[:, rows, :], dst, sem, rx, rc

    for r in range(R):
        src, dst, sem, _, _ = first(r)

        @pl.when(is_self(r))
        def _(src=src, dst=dst, sem=sem):
            pltpu.make_async_copy(src, dst, sem).start()

        @pl.when(jnp.logical_not(is_self(r)))
        def _(src=src, dst=dst, sem=sem, r=r):
            pltpu.make_async_remote_copy(
                src_ref=src, dst_ref=dst, send_sem=send1.at[r], recv_sem=sem,
                device_id=at(y, relay, R * s + r), device_id_type=pl.DeviceIdType.MESH,
            ).start()

    tile = min(T, 128)

    for i in range(T // tile):
        xf = x_ref[i * tile:(i + 1) * tile, :].astype(jnp.float32)
        ss = jnp.sum(xf * xf, axis=1, keepdims=True)
        ssbuf[m, :, i * tile:(i + 1) * tile] = jnp.transpose(jnp.broadcast_to(ss, (tile, 128)))[:8]

    def share_squares(k):
        return pltpu.make_async_remote_copy(
            src_ref=ssbuf.at[m], dst_ref=ssbuf.at[m], send_sem=send_s.at[k], recv_sem=recv_s.at[m],
            device_id=at(y, s, (m + k) % M), device_id_type=pl.DeviceIdType.MESH)

    for k in range(1, M):
        share_squares(k).start()

    def hand(dy, dx, r2):
        yo, xo = other(dy, dx)
        ref = chunk(y, x, core, r2)
        return pltpu.make_async_remote_copy(
            src_ref=ref, dst_ref=ref, send_sem=send_a.at[dy, dx, r2], recv_sem=recv_a.at[y, x, r2],
            device_id=at(yo, 2 * xo + core, m), device_id_type=pl.DeviceIdType.MESH)

    def pass_on(dy, dx, r2):
        yo, xo = other(dy, dx)
        ref = chunk(yo, xo, core, r2)
        return pltpu.make_async_remote_copy(
            src_ref=ref, dst_ref=ref, send_sem=send_b.at[yo, xo, r2], recv_sem=recv_b.at[yo, xo, r2],
            device_id=at(y, 2 * x + 1 - core, m), device_id_type=pl.DeviceIdType.MESH)

    def send_partial(c):
        return pltpu.make_async_remote_copy(
            src_ref=pbuf.at[c], dst_ref=rbuf.at[m], send_sem=send_p.at[c], recv_sem=recv_p.at[m],
            device_id=at(y, s, c), device_id_type=pl.DeviceIdType.MESH)

    def multiply(c):
        w = jnp.concatenate([wbuf[c, p] for p in range(3)], axis=1)
        part = jnp.dot(x_ref[...], w, preferred_element_type=jnp.float32)

        @pl.when(c == m)
        def _():
            pself[...] = part

        @pl.when(c != m)
        def _():
            pbuf[c] = part.astype(pbuf.dtype)
            send_partial(c).start()

    for r2 in range(R):
        arrived(chunk(y, x, core, r2), recv_a.at[y, x, r2])
        for dy, dx in others:
            hand(dy, dx, r2).start()
        pass_on(0, 0, r2).start()

    def take(dy, dx):
        for r2 in range(R):
            yo, xo = other(dy, dx)
            arrived(chunk(yo, xo, core, r2), recv_a.at[yo, xo, r2])
            pass_on(dy, dx, r2).start()

    def work(dx, mine):
        xo = (x + dx) % X
        core_ = core if mine else 1 - core

        def one(r2, carry):
            if not mine:
                for dy in range(Y):
                    yo = (y + dy) % Y
                    arrived(chunk(yo, xo, core_, r2), recv_b.at[yo, xo, r2])
            multiply(xo + core_ * X + S * r2)
            return carry
        lax.fori_loop(0, R, one, 0)

    for dx in range(X):
        for dy in range(Y):
            if dy or dx:
                take(dy, dx)
        work(dx, True)
        work(dx, False)

    for k in range(1, M):
        c = (m + k) % M
        arrived(ssbuf.at[c], recv_s.at[c])
    total = ssbuf[0]
    for c in range(1, M):
        total = total + ssbuf[c]
    inv = lax.rsqrt(total / (F * M) + 1e-06)
    for k in range(1, M):
        c = (m + k) % M
        arrived(rbuf.at[c], recv_p.at[c])
    for i in range(T // tile):
        rows = slice(i * tile, (i + 1) * tile)

        def add(k, acc):
            return acc + rbuf[(m + k) % M, rows, :].astype(jnp.float32)
        acc = lax.fori_loop(1, M, add, pself[rows, :])
        scale = jnp.transpose(jnp.broadcast_to(inv[0:1, rows], (128, tile)))
        out_ref[rows, :] = acc * jnp.concatenate([scale] * 3, axis=1)

    for r in range(R):
        @pl.when(jnp.logical_not(is_self(r)))
        def _(r=r):
            src = first(r)[0]
            arrived(src, send1.at[r])
    for k in range(1, M):
        share_squares(k).wait_send()
        send_partial((m + k) % M).wait_send()
    for r2 in range(R):
        for dy in range(Y):
            for dx in range(X):
                if dy or dx:
                    hand(dy, dx, r2).wait_send()
                pass_on(dy, dx, r2).wait_send()


def projected(tokens, w_in):
    Y, S, M = (lax.axis_size(a) for a in ("parts", "seq", "mp"))
    T, F = tokens.shape
    X, R = S // 2, M // S
    W = 3 * w_in.shape[2]
    dma = pltpu.SemaphoreType.DMA
    return pl.pallas_call(
        functools.partial(project, Y, S, M),
        out_shape=jax.ShapeDtypeStruct((T, W), jnp.float32),
        in_specs=[pl.BlockSpec(memory_space=pltpu.VMEM), pl.BlockSpec(memory_space=pl.ANY)],
        out_specs=pl.BlockSpec(memory_space=pltpu.VMEM),
        scratch_shapes=[
            pltpu.VMEM((M, 3, F, w_in.shape[2]), jnp.bfloat16),
            pltpu.VMEM((M, T, W), jnp.bfloat16),
            pltpu.VMEM((M, T, W), jnp.bfloat16),
            pltpu.VMEM((T, W), jnp.float32),
            pltpu.VMEM((M, 8, T), jnp.float32),
            dma((R,)), dma((Y, X, R)), dma((Y, X, R)), dma((Y, X, R)), dma((Y, X, R)),
            dma((M,)), dma((M,)), dma((M,)), dma((M,)),
        ],
        compiler_params=pltpu.CompilerParams(
            collective_id=0, has_side_effects=True, vmem_limit_bytes=56 * 2**20),
    )(tokens, w_in)


def shards(tokens, w_in, short_filter, long_filter, skip):
    rows = tokens.shape[0]
    width = w_in.shape[2]
    groups = long_filter.shape[0]
    proj = projected(tokens, w_in).reshape(rows, 3, width)
    margin = FLT + 2
    tail = passed_along(proj[rows - margin :].astype(jnp.bfloat16), "seq", 1).astype(jnp.float32)
    extended = jnp.concatenate([tail, proj], axis=0)
    length = FLT + rows
    sharp = jnp.zeros((length, 3, width), jnp.float32)
    for j in range(3):
        sharp = sharp + short_filter[:, j, :][None] * extended[2 - j : 2 - j + length]
    gated = sharp[:, 1] * sharp[:, 2]
    nblock = rows // FLT
    pieces = gated.reshape(nblock + 1, FLT, width)
    windows = jnp.concatenate([pieces[:-1], pieces[1:]], axis=1).reshape(
        nblock, 2 * FLT, groups, GRP
    )
    lead = jnp.zeros((groups, 1), jnp.float32)
    trail = jnp.zeros((groups, FLT), jnp.float32)
    table = jnp.concatenate([lead, long_filter[:, ::-1], trail], axis=1)
    toeplitz = jnp.tile(table, (1, FLT))[:, : FLT * 2 * FLT].reshape(groups, FLT, 2 * FLT)
    conv = jnp.einsum("gts,bsgk->btgk", toeplitz, windows, precision=lax.Precision.HIGHEST)
    filtered = conv.reshape(rows, width) + skip[None, :] * gated[FLT:]
    return (sharp[FLT:, 0] * filtered).astype(jnp.bfloat16)


def solution(mesh):
    return jax.shard_map(
        shards,
        mesh=mesh,
        in_specs=(
            P(("parts", "seq"), "mp"),
            P(None, "seq", "mp"),
            P(None, None, "mp"),
            P("mp", None),
            P("mp"),
        ),
        out_specs=P(("parts", "seq"), "mp"),
        check_vma=False,
    )
```

```python
import functools

import jax
import jax.numpy as jnp
from jax import lax
from jax.experimental import pallas as pl
from jax.experimental.pallas import tpu as pltpu
from jax.sharding import PartitionSpec as P

FLT = 128
GRP = 16


def passed_along(block, axis, distance):
    devices = range(lax.axis_size(axis))
    route = [(i - distance, i) for i in devices if i - distance in devices]
    return lax.ppermute(block, axis, route)


def project(Y, S, M, x_ref, w_ref, out_ref, wbuf, pbuf, rbuf, pself, ssbuf,
            send1, send_a, recv_a, send_b, recv_b, send_p, recv_p, send_s, recv_s):
    X, R = S // 2, M // S
    T, F = x_ref.shape
    part_rows = F // Y
    y, s, m = lax.axis_index("parts"), lax.axis_index("seq"), lax.axis_index("mp")
    x, core = s // 2, s % 2

    def at(y_, s_, m_):
        return {"parts": y_, "seq": s_, "mp": m_}

    mq = m % S
    relay = 2 * (mq % X) + mq // X
    family = x + core * X

    def is_self(r):
        return jnp.logical_and(relay == s, R * s + r == m)

    def source_is_self(r2):
        return jnp.logical_and(m // R == s, family + S * r2 == m)

    def chunk(y_, x_, core_, r2, p):
        c = x_ + core_ * X + S * r2
        return wbuf.at[c, p, pl.ds(pl.multiple_of(y_ * part_rows, part_rows), part_rows), :]

    def arrived(ref, sem):
        pltpu.make_async_copy(ref, ref, sem).wait()

    others = [(dy, dx) for dx in range(X) for dy in range(Y) if dy or dx]

    def other(dy, dx):
        return (y + dy) % Y, (x + dx) % X

    barrier = pltpu.get_barrier_semaphore()

    def greet(dev):
        pl.semaphore_signal(barrier, inc=1, device_id=dev, device_id_type=pl.DeviceIdType.MESH)

    for r in range(R):
        @pl.when(jnp.logical_not(is_self(r)))
        def _(r=r):
            greet(at(y, relay, R * s + r))

        @pl.when(jnp.logical_not(source_is_self(r)))
        def _(r=r):
            greet(at(y, m // R, family + S * r))
    for dy, dx in others:
        yo, xo = other(dy, dx)
        greet(at(yo, 2 * xo + core, m))
    greet(at(y, 2 * x + 1 - core, m))
    for k in range(1, M):
        greet(at(y, s, (m + k) % M))
    peers = len(others) + 1 + M - 1 + 2 * R
    for r in range(R):
        peers = peers - is_self(r).astype(jnp.int32) - source_is_self(r).astype(jnp.int32)
    pl.semaphore_wait(barrier, peers)

    def first(r, p):
        rows = pl.ds(pl.multiple_of(r * F + y * part_rows, part_rows), part_rows)
        dst = wbuf.at[m, p, pl.ds(pl.multiple_of(y * part_rows, part_rows), part_rows), :]
        rx = relay // 2
        sem = recv_a.at[y, rx, m // S, p]
        return w_ref.at[p, rows, :], dst, sem

    for p, r in [(p, r) for p in range(3) for r in range(R)]:
        src, dst, sem = first(r, p)

        @pl.when(is_self(r))
        def _(src=src, dst=dst, sem=sem):
            pltpu.make_async_copy(src, dst, sem).start()

        @pl.when(jnp.logical_not(is_self(r)))
        def _(src=src, dst=dst, sem=sem, r=r, p=p):
            pltpu.make_async_remote_copy(
                src_ref=src, dst_ref=dst, send_sem=send1.at[r, p], recv_sem=sem,
                device_id=at(y, relay, R * s + r), device_id_type=pl.DeviceIdType.MESH,
            ).start()

    tile = min(T, 128)

    for i in range(T // tile):
        xf = x_ref[i * tile:(i + 1) * tile, :].astype(jnp.float32)
        ss = jnp.sum(xf * xf, axis=1, keepdims=True)
        ssbuf[m, :, i * tile:(i + 1) * tile] = jnp.transpose(jnp.broadcast_to(ss, (tile, 128)))[:8]

    def share_squares(k):
        return pltpu.make_async_remote_copy(
            src_ref=ssbuf.at[m], dst_ref=ssbuf.at[m], send_sem=send_s.at[k], recv_sem=recv_s.at[m],
            device_id=at(y, s, (m + k) % M), device_id_type=pl.DeviceIdType.MESH)

    for k in range(1, M):
        share_squares(k).start()

    def hand(dy, dx, r2, p):
        yo, xo = other(dy, dx)
        ref = chunk(y, x, core, r2, p)
        return pltpu.make_async_remote_copy(
            src_ref=ref, dst_ref=ref, send_sem=send_a.at[dy, dx, r2, p], recv_sem=recv_a.at[y, x, r2, p],
            device_id=at(yo, 2 * xo + core, m), device_id_type=pl.DeviceIdType.MESH)

    def pass_on(dy, dx, r2, p):
        yo, xo = other(dy, dx)
        ref = chunk(yo, xo, core, r2, p)
        return pltpu.make_async_remote_copy(
            src_ref=ref, dst_ref=ref, send_sem=send_b.at[yo, xo, r2, p], recv_sem=recv_b.at[yo, xo, r2, p],
            device_id=at(y, 2 * x + 1 - core, m), device_id_type=pl.DeviceIdType.MESH)

    def send_partial(c, p):
        return pltpu.make_async_remote_copy(
            src_ref=pbuf.at[c, p], dst_ref=rbuf.at[m, p], send_sem=send_p.at[c, p],
            recv_sem=recv_p.at[m, p],
            device_id=at(y, s, c), device_id_type=pl.DeviceIdType.MESH)

    def multiply(c, p):
        part = jnp.dot(x_ref[...], wbuf[c, p], preferred_element_type=jnp.float32)

        @pl.when(c == m)
        def _():
            pself[p] = part

        @pl.when(c != m)
        def _():
            pbuf[c, p] = part.astype(pbuf.dtype)
            send_partial(c, p).start()

    def give(p):
        for r2 in range(R):
            arrived(chunk(y, x, core, r2, p), recv_a.at[y, x, r2, p])
            for dy, dx in others:
                hand(dy, dx, r2, p).start()
            pass_on(0, 0, r2, p).start()

    def take(dy, dx, p):
        for r2 in range(R):
            yo, xo = other(dy, dx)
            arrived(chunk(yo, xo, core, r2, p), recv_a.at[yo, xo, r2, p])
            pass_on(dy, dx, r2, p).start()

    def work(dx, mine, p):
        xo = (x + dx) % X
        core_ = core if mine else 1 - core

        def one(r2, carry):
            if not mine:
                for dy in range(Y):
                    yo = (y + dy) % Y
                    arrived(chunk(yo, xo, core_, r2, p), recv_b.at[yo, xo, r2, p])
            multiply(xo + core_ * X + S * r2, p)
            return carry
        lax.fori_loop(0, R, one, 0)

    give(0)
    for p in range(3):
        if p < 2:
            give(p + 1)
        for dx in range(X):
            for dy in range(Y):
                if dy or dx:
                    take(dy, dx, p)
            work(dx, True, p)
            work(dx, False, p)

    for k in range(1, M):
        c = (m + k) % M
        arrived(ssbuf.at[c], recv_s.at[c])
    total = ssbuf[0]
    for c in range(1, M):
        total = total + ssbuf[c]
    inv = lax.rsqrt(total / (F * M) + 1e-06)
    for p in range(3):
        for k in range(1, M):
            c = (m + k) % M
            arrived(rbuf.at[c, p], recv_p.at[c, p])
        for i in range(T // tile):
            rows = slice(i * tile, (i + 1) * tile)

            def add(k, acc):
                return acc + rbuf[(m + k) % M, p, rows, :].astype(jnp.float32)
            acc = lax.fori_loop(1, M, add, pself[p, rows, :])
            scale = jnp.transpose(jnp.broadcast_to(inv[0:1, rows], (128, tile)))
            out_ref[rows, p * 128:(p + 1) * 128] = acc * scale

    for k in range(1, M):
        share_squares(k).wait_send()
    for p in range(3):
        for r in range(R):
            @pl.when(jnp.logical_not(is_self(r)))
            def _(r=r, p=p):
                arrived(first(r, p)[0], send1.at[r, p])
        for k in range(1, M):
            send_partial((m + k) % M, p).wait_send()
        for r2 in range(R):
            for dy in range(Y):
                for dx in range(X):
                    if dy or dx:
                        hand(dy, dx, r2, p).wait_send()
                    pass_on(dy, dx, r2, p).wait_send()


def projected(tokens, w_in):
    Y, S, M = (lax.axis_size(a) for a in ("parts", "seq", "mp"))
    T, F = tokens.shape
    X, R = S // 2, M // S
    W = 3 * w_in.shape[2]
    dma = pltpu.SemaphoreType.DMA
    return pl.pallas_call(
        functools.partial(project, Y, S, M),
        out_shape=jax.ShapeDtypeStruct((T, W), jnp.float32),
        in_specs=[pl.BlockSpec(memory_space=pltpu.VMEM), pl.BlockSpec(memory_space=pl.ANY)],
        out_specs=pl.BlockSpec(memory_space=pltpu.VMEM),
        scratch_shapes=[
            pltpu.VMEM((M, 3, F, w_in.shape[2]), jnp.bfloat16),
            pltpu.VMEM((M, 3, T, W // 3), jnp.bfloat16),
            pltpu.VMEM((M, 3, T, W // 3), jnp.bfloat16),
            pltpu.VMEM((3, T, W // 3), jnp.float32),
            pltpu.VMEM((M, 8, T), jnp.float32),
            dma((R, 3)), dma((Y, X, R, 3)), dma((Y, X, R, 3)), dma((Y, X, R, 3)), dma((Y, X, R, 3)),
            dma((M, 3)), dma((M, 3)), dma((M,)), dma((M,)),
        ],
        compiler_params=pltpu.CompilerParams(
            collective_id=0, has_side_effects=True, vmem_limit_bytes=56 * 2**20),
    )(tokens, w_in)


def shards(tokens, w_in, short_filter, long_filter, skip):
    rows = tokens.shape[0]
    width = w_in.shape[2]
    groups = long_filter.shape[0]
    proj = projected(tokens, w_in).reshape(rows, 3, width)
    margin = FLT + 2
    tail = passed_along(proj[rows - margin :].astype(jnp.bfloat16), "seq", 1).astype(jnp.float32)
    extended = jnp.concatenate([tail, proj], axis=0)
    length = FLT + rows
    sharp = jnp.zeros((length, 3, width), jnp.float32)
    for j in range(3):
        sharp = sharp + short_filter[:, j, :][None] * extended[2 - j : 2 - j + length]
    gated = sharp[:, 1] * sharp[:, 2]
    nblock = rows // FLT
    pieces = gated.reshape(nblock + 1, FLT, width)
    windows = jnp.concatenate([pieces[:-1], pieces[1:]], axis=1).reshape(
        nblock, 2 * FLT, groups, GRP
    )
    lead = jnp.zeros((groups, 1), jnp.float32)
    trail = jnp.zeros((groups, FLT), jnp.float32)
    table = jnp.concatenate([lead, long_filter[:, ::-1], trail], axis=1)
    toeplitz = jnp.tile(table, (1, FLT))[:, : FLT * 2 * FLT].reshape(groups, FLT, 2 * FLT)
    conv = jnp.einsum("gts,bsgk->btgk", toeplitz, windows, precision=lax.Precision.HIGHEST)
    filtered = conv.reshape(rows, width) + skip[None, :] * gated[FLT:]
    return (sharp[FLT:, 0] * filtered).astype(jnp.bfloat16)


def solution(mesh):
    return jax.shard_map(
        shards,
        mesh=mesh,
        in_specs=(
            P(("parts", "seq"), "mp"),
            P(None, "seq", "mp"),
            P(None, None, "mp"),
            P("mp", None),
            P("mp"),
        ),
        out_specs=P(("parts", "seq"), "mp"),
        check_vma=False,
    )
```
